1024 devices in a mesh: dp: 8 (over y), lat: 16 (over z_lo, core), lon: 8 (over z_hi, x).
Axes of the slice: x: 4, y: 8, z: 16 (z_hi: 2, z_lo: 8; z = z_hi * 8 + z_lo), core: 2. Of those that a mesh axis runs over, the one named last changes fastest.
Arguments:
- field: bfloat16 [8, 128, 512, 384], P('dp', 'lat', 'lon'), may hold values from -6 to 6
- cotangent: bfloat16 [8, 128, 512, 384], P('dp', 'lat', 'lon'), may hold values from -6 to 6
- spectral_weight: bfloat16 [512, 128, 2, 512], P('dp', ('lat', 'lon')), may hold values from -0.1875 to 0.1875
Outputs:
- grad_input: bfloat16 [8, 128, 512, 384], P('dp', 'lat', 'lon')
- grad_weight: bfloat16 [512, 128, 2, 512], P('dp', ('lat', 'lon'))
The draws below stay inside these ranges and needn't reach their ends.
All inputs are finite; a program needn't handle non-finite values.
Results may differ from the reference program's by a relative error of at most 0.019.
Values may be sent and summed in bfloat16 or wider, within the bound.
A program may use at most 32 MiB of HBM per device.

```python
import math
import jax
import jax.numpy as jnp
from jax import lax

E = 512
NLON = 384
SAMPLES = 8
NLAT = 128
DEGREES = 128
ORDERS = 64


def strengthened(result, stream_key, source, target, parts, factor):
    def block_of(position):
        return (jnp.arange(result.shape[position]) // (result.shape[position] // parts)).reshape((-1,) + (1,) * (result.ndim - 1 - position))

    near = jax.random.permutation(stream_key, parts)[block_of(target)]
    other_side = (block_of(target) + parts // 2) % parts
    return jnp.where((block_of(source) == near) | (block_of(source) == other_side), factor * result, result)


def steps_of(stream_key, extent, pieces, smallest, largest):
    level = 1.0
    for dim, parts in pieces:
        heights = jax.random.uniform(jax.random.fold_in(jax.random.fold_in(stream_key, 6), dim), (parts,), jnp.float32, smallest / len(pieces), largest / len(pieces))
        level = level * jnp.repeat(jnp.exp(heights), extent[dim] // parts).reshape((-1,) + (1,) * (len(extent) - 1 - dim))
    return level


def scatter_about(rng, extent, deviation, bound, pieces=(), kind=jnp.bfloat16):
    array = jax.random.normal(rng, extent, jnp.float32) * deviation
    if len(pieces) > 0:
        array = steps_of(rng, extent, pieces, -0.22, 0.18) * array
    return jnp.clip(array, min=-bound, max=bound).astype(kind)


def gaussian_with(rng, extent, scale, reach, cuts, heavy, kind=jnp.bfloat16):
    result = scale * jax.random.normal(rng, extent, jnp.float32)
    if cuts:
        result = result * steps_of(rng, extent, cuts, -0.22, 0.18)
    return jnp.clip(strengthened(result, jax.random.fold_in(rng, 3), *heavy), -reach, reach).astype(kind)


def setup_inputs(seed: int = 0) -> dict:
    key_list = jax.random.split(jax.random.key(seed), 4)
    return {
        "field": gaussian_with(key_list[0], (SAMPLES, NLAT, E, NLON), 1.0, 6.0, ((0, 8), (1, 16), (2, 8)), (0, 2, 8, 2.0)),
        "cotangent": scatter_about(key_list[1], (SAMPLES, NLAT, E, NLON), 1.0, 6.0, ((0, 8), (1, 16), (2, 8))),
        "spectral_weight": scatter_about(key_list[2], (E, DEGREES, 2, E), (2 * E) ** -0.5, 0.1875, ((0, 8), (1, 128))),
    }


def rounded(values):
    return lax.optimization_barrier(values.astype(jnp.bfloat16)).astype(jnp.float32)

def fourier_tables(nlon, norders):
    cols = jnp.arange(nlon, dtype=jnp.int32)[:, None]
    rows = jnp.arange(norders, dtype=jnp.int32)[None, :]
    phase = (cols * rows % nlon).astype(jnp.float32) * (2.0 * math.pi / nlon)
    cosine = jnp.cos(phase)
    sine = jnp.sin(phase)
    doubled = jnp.where(rows == 0, 1.0, 2.0).astype(jnp.float32)
    forward = jnp.stack([cosine / nlon, -sine / nlon], axis=-1)
    inverse = jnp.stack([doubled * cosine, -doubled * sine], axis=-1)
    return (forward, inverse)

def quad_weights(nlat):
    theta = math.pi * (jnp.arange(nlat, dtype=jnp.float32) + 0.5) / nlat
    return math.pi * jnp.sin(theta) / nlat

def legendre_rows(orders, nlat, ndeg):
    theta = math.pi * (jnp.arange(nlat, dtype=jnp.float32) + 0.5) / nlat
    cosine = jnp.cos(theta)[None, :]
    sine = jnp.sin(theta)[None, :]
    order_f = orders.astype(jnp.float32)[:, None]
    log_start = 0.5 * math.log(0.5) + 0.5 * (lax.lgamma(2.0 * order_f + 2.0) - order_f * math.log(4.0) - 2.0 * lax.lgamma(order_f + 1.0)) + order_f * jnp.log(sine)
    start = jnp.exp(log_start)

    def advance(carry, degree):
        older, newer = carry
        deg = degree.astype(jnp.float32)
        scale_a = jnp.sqrt(jnp.maximum(4.0 * deg * deg - 1.0, 0.0) / jnp.maximum(deg * deg - order_f * order_f, 1.0))
        scale_b = jnp.sqrt(jnp.maximum((deg - 1.0) ** 2 - order_f * order_f, 0.0) / jnp.maximum(4.0 * (deg - 1.0) ** 2 - 1.0, 1.0))
        general = scale_a * (cosine * newer - scale_b * older)
        value = jnp.where(deg < order_f, 0.0, jnp.where(deg == order_f, start, general))
        return ((newer, value), value)
    zeros = jnp.zeros(start.shape, jnp.float32)
    _, table = lax.scan(advance, (zeros, zeros), jnp.arange(ndeg, dtype=jnp.int32), unroll=16)
    return jnp.transpose(table, (1, 0, 2))

def gelu_slope(values):
    return 0.5 * (1.0 + lax.erf(values * (1.0 / math.sqrt(2.0)))) + values * jnp.exp(-0.5 * values * values) * (1.0 / math.sqrt(2.0 * math.pi))

def reference(field, cotangent, spectral_weight):
    nlat = field.shape[1]
    nlon = field.shape[3]
    forward_tab, inverse_tab = fourier_tables(nlon, ORDERS)
    forward_tab = rounded(forward_tab)
    inverse_tab = rounded(inverse_tab)
    legendre = legendre_rows(jnp.arange(ORDERS, dtype=jnp.int32), nlat, DEGREES)
    analysis_leg = rounded(legendre * quad_weights(nlat)[None, None, :])
    synthesis_leg = rounded(legendre)
    weight_full = spectral_weight.astype(jnp.float32)

    def per_sample(total, pair):
        grid, grad_out = pair
        grad_out = grad_out.astype(jnp.float32)
        spectrum = rounded(jnp.einsum('ten,nmc->mtce', grid.astype(jnp.float32), forward_tab))
        coeff = rounded(jnp.einsum('mlt,mtce->lmce', analysis_leg, spectrum))
        product = jnp.einsum('lmce,eldo->lmcdo', coeff, weight_full)
        mixed = rounded(jnp.stack([product[:, :, 0, 0] - product[:, :, 1, 1], product[:, :, 0, 1] + product[:, :, 1, 0]], axis=2))
        grid_spec = rounded(jnp.einsum('mlt,lmce->mtce', synthesis_leg, mixed))
        filtered = jnp.einsum('mtce,nmc->ten', grid_spec, inverse_tab)
        filtered_grad = rounded(grad_out * gelu_slope(filtered))
        grad_spec = rounded(jnp.einsum('ten,nmc->mtce', filtered_grad, inverse_tab))
        mixed_grad = rounded(jnp.einsum('mlt,mtce->lmce', synthesis_leg, grad_spec))
        turned = jnp.stack([-coeff[:, :, 1], coeff[:, :, 0]], axis=2)
        paired = jnp.stack([coeff, turned], axis=2)
        term = jnp.einsum('lmdce,lmco->eldo', paired, mixed_grad)
        back = jnp.einsum('lmco,eldo->lmcde', mixed_grad, weight_full)
        coeff_grad = rounded(jnp.stack([back[:, :, 0, 0] + back[:, :, 1, 1], back[:, :, 1, 0] - back[:, :, 0, 1]], axis=2))
        spec_grad = rounded(jnp.einsum('mlt,lmce->mtce', analysis_leg, coeff_grad))
        grad_in = (grad_out + jnp.einsum('mtce,nmc->ten', spec_grad, forward_tab)).astype(jnp.bfloat16)
        return (total + term, grad_in)
    start_total = jnp.zeros((E, DEGREES, 2, E), jnp.float32)
    total, grads = lax.scan(per_sample, start_total, (field, cotangent))
    return (grads, (total * (1.0 / SAMPLES)).astype(jnp.bfloat16))
```

```python
import functools
import math

import jax
import jax.numpy as jnp
import numpy as np
from jax import lax
from jax.experimental import pallas as pl
from jax.experimental.pallas import tpu as pltpu
from jax.sharding import PartitionSpec as P

MESH = pl.DeviceIdType.MESH
BF16 = jnp.bfloat16
F32 = jnp.float32
M_DEV = 4
ROWS = 8
SLAB = 64
N_EXCHANGES = 8
SEM_WEIGHTS, SEM_COEFF, SEM_GRADS = 8, 9, 10


def fourier_tables(nlon, norders):
    cols = np.arange(nlon, dtype=np.int32)[None, :]
    rows = np.arange(norders, dtype=np.int32)[:, None]
    phase = (cols * rows % nlon).astype(np.float32) * np.float32(2.0 * math.pi / nlon)
    cosine, sine = np.cos(phase), np.sin(phase)
    doubled = np.where(rows == 0, 1.0, 2.0).astype(np.float32)
    forward = np.concatenate([cosine / np.float32(nlon), -sine / np.float32(nlon)])
    inverse = np.concatenate([doubled * cosine, -doubled * sine])
    return jnp.asarray(forward, BF16), jnp.asarray(inverse, BF16)


def legendre_seeds(nlat, norders):
    theta = np.float32(math.pi) * (np.arange(nlat, dtype=np.float32) + np.float32(0.5)) / np.float32(nlat)
    theta = theta.astype(np.float64)
    seeds = np.zeros((norders // M_DEV, 8, nlat), np.float32)
    for m in range(norders):
        scale = math.lgamma(2.0 * m + 2.0) - m * math.log(4.0) - 2.0 * math.lgamma(m + 1.0)
        start = 0.5 * math.log(0.5) + 0.5 * scale + m * np.log(np.sin(theta))
        seeds[m // M_DEV, m % M_DEV] = np.exp(start).astype(np.float32)
    rows = np.zeros((8, nlat), np.float32)
    rows[0] = np.cos(theta)
    rows[1] = math.pi * np.sin(theta) / nlat
    return jnp.asarray(seeds.reshape(-1, nlat)), jnp.asarray(rows)


def swap_halves(tile):
    return pltpu.roll(tile, 64, axis=1)


def low_lanes(shape):
    return lax.broadcasted_iota(jnp.int32, shape, 1) < 64


def gelu_slope(values):
    return 0.5 * (1.0 + lax.erf(values * (1.0 / math.sqrt(2.0)))) + values * jnp.exp(
        -0.5 * values * values
    ) * (1.0 / math.sqrt(2.0 * math.pi))


def kernel(
    sizes,
    x_ref,
    g_ref,
    w_ref,
    forward_ref,
    inverse_ref,
    seeds_ref,
    rows_ref,
    out_ref,
    gw_ref,
    by_lat_out,
    by_lat_in,
    by_deg_out,
    by_deg_in,
    wide,
    coeff_all,
    grads_all,
    mixing,
    hbuf,
    fgrad,
    stage,
    leg,
    analysis,
    analysis_t,
    synthesis,
    synthesis_t,
    send_sem,
    recv_sem,
):
    n_dp, n_lat, n_lon = sizes
    n_x = min(n_lon, 4)
    n_zlo = n_lat // 2
    n_z = n_zlo * (n_lon // n_x)
    orders = n_lat * M_DEV
    n_deg = n_lat * n_lon
    nlat = n_lat * ROWS
    mrows = orders
    s = lax.axis_index("dp")
    a = lax.axis_index("lat")
    y = lax.axis_index("lon")
    chip, core = lax.div(a, 2), lax.rem(a, 2)
    x, zhi = lax.rem(y, n_x), lax.div(y, n_x)
    z = zhi * n_zlo + chip

    def over_degree_group(visit):
        def step(k, carry):
            half = lax.div(k + 1, 2)
            off = jnp.where(lax.rem(k, 2) == 1, n_z // 2 - half, n_z // 2 + half)
            zt = lax.rem(z + off, n_z)
            zl, zh = lax.rem(zt, n_zlo), lax.div(zt, n_zlo)
            for dx in list(range(n_x // 2, 0, -1)) + list(range(n_x // 2 + 1, n_x)) + [0]:
                for dc in (1, 0):
                    la = zl * 2 + lax.rem(core + dc, 2)
                    lo = zh * n_x + lax.rem(x + dx, n_x)
                    if dx == 0 and dc == 0:
                        pl.when(k < n_z - 1)(functools.partial(visit, la, lo))
                    else:
                        visit(la, lo)
            return carry

        lax.fori_loop(0, n_z, step, 0)

    def over_lat_group(visit):
        for d in range(n_zlo - 1, 0, -1):
            for q in (chip + d, chip - d):

                @pl.when((q >= 0) & (q < n_zlo))
                def _(q=q):
                    visit(q * 2)
                    visit(q * 2 + 1)

        visit(chip * 2 + 1 - core)

    def over_dp_group(visit):
        for d in list(range(n_dp // 2, 0, -1)) + list(range(n_dp // 2 + 1, n_dp)):
            visit(lax.rem(s + d, n_dp))

    def remote(src, dst, sem, device):
        pltpu.make_async_remote_copy(
            src_ref=src,
            dst_ref=dst,
            send_sem=send_sem.at[sem],
            recv_sem=recv_sem.at[sem],
            device_id=device,
            device_id_type=MESH,
        ).start()

    def local(src, dst, sem):
        pltpu.make_async_copy(src, dst, recv_sem.at[sem]).start()

    def arrived(ref, sem):
        pltpu.make_async_copy(ref, ref, recv_sem.at[sem]).wait()

    def sent(ref, sem):
        pltpu.make_async_copy(ref, ref, send_sem.at[sem]).wait()

    def send_by_lat(e, k):
        src, dst = by_lat_out.at[k], by_lat_in.at[k]
        over_lat_group(lambda j: remote(src.at[j], dst.at[a], e, {"lat": j}))
        local(src.at[a], dst.at[a], e)

    def send_to_degrees(e, k):
        src, dst = by_deg_out.at[k], by_deg_in.at[k]
        mine = y * n_lat + a
        over_degree_group(
            lambda la, lo: remote(src.at[la * n_lon + lo], dst.at[mine], e, {"lat": la, "lon": lo})
        )
        local(src.at[a * n_lon + y], dst.at[mine], e)

    def send_to_orders(e, k):
        src, dst = by_deg_out.at[k], by_deg_in.at[k]
        mine = a * n_lon + y
        over_degree_group(
            lambda la, lo: remote(src.at[lo * n_lat + la], dst.at[mine], e, {"lat": la, "lon": lo})
        )
        local(src.at[y * n_lat + a], dst.at[mine], e)

    def to_spectrum(table, values, k):
        out = lax.dot_general(
            table, values, (((1,), (1,)), ((), ())), preferred_element_type=F32
        )
        low = low_lanes((orders, 128))
        for j in range(ROWS // 2):
            real = out[:orders, j * 128 : (j + 1) * 128]
            imag = out[orders:, j * 128 : (j + 1) * 128]
            stage[pl.ds(2 * j, orders, stride=ROWS), :] = jnp.where(low, real, swap_halves(imag))
            stage[pl.ds(2 * j + 1, orders, stride=ROWS), :] = jnp.where(low, swap_halves(real), imag)
        by_lat_out[k] = stage[: orders * ROWS, :].astype(BF16).reshape(n_lat, M_DEV * ROWS, 128)

    def to_degrees(tables, k_in, k):
        for m in range(M_DEV):
            part = by_lat_in[k_in, :, m * ROWS : (m + 1) * ROWS, :]
            part = part.astype(F32).reshape(nlat, 128).astype(BF16)
            stage[pl.ds(m, n_deg, stride=M_DEV), :] = jnp.dot(
                tables[m], part, preferred_element_type=F32
            )
        by_deg_out[k] = stage[: n_deg * M_DEV, :].reshape(n_deg, M_DEV, 128).astype(BF16)

    def gather_wide(k):
        for j in range(n_lon):
            part = by_deg_in[k, j * n_lat : (j + 1) * n_lat]
            wide[:, j * 128 : (j + 1) * 128] = part.astype(F32).reshape(mrows, 128).astype(BF16)

    def scatter_wide(value, k):
        for j in range(n_lon):
            part = value[:, j * 128 : (j + 1) * 128].reshape(n_lat, M_DEV, 128)
            by_deg_out[k, j * n_lat : (j + 1) * n_lat] = part.astype(BF16)

    def to_rows(tables, k_in, k):
        stage[: n_deg * M_DEV, :] = by_deg_in[k_in].astype(F32).reshape(n_deg * M_DEV, 128)
        parts = []
        for m in range(M_DEV):
            part = stage[pl.ds(m, n_deg, stride=M_DEV), :].astype(BF16)
            out = jnp.dot(tables[m], part, preferred_element_type=F32)
            parts.append(out.reshape(n_lat, ROWS, 128))
        both = jnp.stack(parts, axis=1).reshape(n_lat, M_DEV * ROWS, 128)
        by_lat_out[k] = both.astype(BF16)

    def to_grid(table_ref, k, use):
        stage[: orders * ROWS, :] = by_lat_in[k].astype(F32).reshape(orders * ROWS, 128)
        low = low_lanes((orders, 128))
        for j in range(ROWS // 2):
            even = stage[pl.ds(2 * j, orders, stride=ROWS), :]
            odd = stage[pl.ds(2 * j + 1, orders, stride=ROWS), :]
            real = jnp.where(low, even, swap_halves(odd))
            imag = jnp.where(low, swap_halves(even), odd)
            both = jnp.concatenate([real, imag], axis=0).astype(BF16)
            use(
                slice(j * 128, (j + 1) * 128),
                lax.dot_general(
                    both, table_ref[...], (((0,), (0,)), ((), ())), preferred_element_type=F32
                ),
            )

    barrier = pltpu.get_barrier_semaphore()

    def greet(device):
        pl.semaphore_signal(barrier, inc=1, device_id=device, device_id_type=MESH)

    over_degree_group(lambda la, lo: greet({"lat": la, "lon": lo}))
    over_dp_group(lambda j: greet({"dp": j}))

    to_spectrum(forward_ref[...], x_ref[...], 0)
    pl.semaphore_wait(barrier, n_deg - 1 + n_dp - 1)

    send_by_lat(0, 0)
    own_rows = pl.ds(pl.multiple_of(s * 128, 128), 64)
    over_dp_group(lambda j: remote(w_ref, mixing.at[own_rows, :], SEM_WEIGHTS, {"dp": j}))
    local(w_ref, mixing.at[own_rows, :], SEM_WEIGHTS)

    order = (a * M_DEV + lax.broadcasted_iota(jnp.int32, (8, nlat), 0)).astype(F32)
    order_sq = order * order
    cosine = jnp.broadcast_to(rows_ref[0:1, :], (8, nlat))
    start = seeds_ref[pl.ds(pl.multiple_of(a * 8, 8), 8), :]

    def advance(degree, carry):
        older, newer, deg = carry
        below = deg - 1.0
        scale_a = jnp.sqrt(
            jnp.maximum(4.0 * deg * deg - 1.0, 0.0) / jnp.maximum(deg * deg - order_sq, 1.0)
        )
        scale_b = jnp.sqrt(
            jnp.maximum(below * below - order_sq, 0.0)
            / jnp.maximum(4.0 * (below * below) - 1.0, 1.0)
        )
        general = scale_a * (cosine * newer - scale_b * older)
        value = jnp.where(deg < order, 0.0, jnp.where(deg == order, start, general))
        leg[pl.ds(pl.multiple_of(degree * 8, 8), 8), :] = value
        return newer, value, deg + 1.0

    zeros = start * 0.0
    lax.fori_loop(0, n_deg, advance, (zeros, zeros, zeros), unroll=8)
    for m in range(M_DEV):
        table = leg[pl.ds(m, n_deg, stride=8), :]
        weighted = table * rows_ref[1:2, :]
        synthesis[m] = table.astype(BF16)
        analysis[m] = weighted.astype(BF16)
        synthesis_t[m] = table.T.astype(BF16)
        analysis_t[m] = weighted.T.astype(BF16)

    arrived(by_lat_in.at[0], 0)
    to_degrees(analysis, 0, 0)
    send_to_degrees(1, 0)

    arrived(wide_shape(mixing, n_lon), SEM_WEIGHTS)
    low = low_lanes((64, 128))
    for j in range(n_lon):
        for i in range(n_lon):
            turned = swap_halves(mixing[j * 128 : j * 128 + 64, i * 128 : (i + 1) * 128].astype(F32))
            mixing[j * 128 + 64 : (j + 1) * 128, i * 128 : (i + 1) * 128] = jnp.where(
                low, -turned, turned
            ).astype(BF16)

    arrived(by_deg_in.at[0], 1)
    gather_wide(0)
    scatter_wide(jnp.dot(wide[...], mixing[...], preferred_element_type=F32), 1)
    send_to_orders(2, 1)

    def coeff_block(j):
        return by_deg_in.at[0, pl.ds(j * n_lat, n_lat)]

    over_dp_group(lambda j: remote(coeff_block(j), coeff_all.at[s], SEM_COEFF, {"dp": j}))
    local(coeff_block(s), coeff_all.at[s], SEM_COEFF)

    arrived(by_deg_in.at[1], 2)
    to_rows(synthesis_t, 1, 1)
    send_by_lat(3, 1)
    arrived(by_lat_in.at[1], 3)

    def slope(rows, filtered):
        fgrad[rows, :] = (g_ref[rows, :].astype(F32) * gelu_slope(filtered)).astype(BF16)

    to_grid(inverse_ref, 1, slope)
    to_spectrum(inverse_ref[...], fgrad[...], 2)
    send_by_lat(4, 2)
    arrived(by_lat_in.at[2], 4)
    to_degrees(synthesis, 2, 2)
    send_to_degrees(5, 2)
    arrived(by_deg_in.at[2], 5)

    gather_wide(2)
    over_dp_group(lambda j: remote(by_deg_in.at[2], grads_all.at[s], SEM_GRADS, {"dp": j}))
    local(by_deg_in.at[2], grads_all.at[s], SEM_GRADS)
    scatter_wide(
        lax.dot_general(
            wide[...], mixing[...], (((1,), (1,)), ((), ())), preferred_element_type=F32
        ),
        3,
    )
    send_to_orders(6, 3)
    arrived(by_deg_in.at[3], 6)
    to_rows(analysis_t, 3, 3)
    send_by_lat(7, 3)
    arrived(by_lat_in.at[3], 7)

    def finish(rows, branch):
        out_ref[rows, :] = (g_ref[rows, :].astype(F32) + branch).astype(BF16)

    to_grid(forward_ref, 3, finish)

    arrived(coeff_all, SEM_COEFF)
    arrived(grads_all, SEM_GRADS)
    for i in range(n_dp):
        for j in range(n_lon):
            part = grads_all[i, j * n_lat : (j + 1) * n_lat]
            hbuf[i * mrows : (i + 1) * mrows, j * 128 : (j + 1) * 128] = (
                part.astype(F32).reshape(mrows, 128).astype(BF16)
            )
    parts = coeff_all[...].astype(F32).reshape(n_dp * mrows, 128).astype(BF16)
    total = lax.dot_general(
        parts, hbuf[...], (((0,), (0,)), ((), ())), preferred_element_type=F32
    )
    for j in range(n_lon):
        real = total[:64, j * 128 : (j + 1) * 128]
        imag = swap_halves(total[64:, j * 128 : (j + 1) * 128])
        gw_ref[:, j * 128 : (j + 1) * 128] = (
            jnp.where(low, real + imag, real - imag) * (1.0 / n_dp)
        ).astype(BF16)

    for e, k in ((0, 0), (3, 1), (4, 2), (7, 3)):
        sent(by_lat_out.at[k, pl.ds(0, n_lat - 1)], e)
    for e, k in ((1, 0), (2, 1), (5, 2), (6, 3)):
        sent(by_deg_out.at[k, pl.ds(0, n_deg - 1)], e)
    sent(coeff_all.at[pl.ds(0, n_dp - 1)], SEM_COEFF)
    sent(grads_all.at[pl.ds(0, n_dp - 1)], SEM_GRADS)
    sent(mixing.at[pl.ds(0, 64 * (n_dp - 1)), :], SEM_WEIGHTS)


def wide_shape(mixing, n_lon):
    return mixing.at[pl.ds(0, 64 * n_lon), :]


def body(sizes, field, cotangent, spectral_weight):
    n_dp, n_lat, n_lon = sizes
    nlon = field.shape[3]
    orders, n_deg, nlat = n_lat * M_DEV, n_lat * n_lon, n_lat * ROWS
    width = n_lon * 128
    rows = ROWS * SLAB
    forward, inverse = fourier_tables(nlon, orders)
    seeds, lat_rows = legendre_seeds(nlat, orders)
    weights = spectral_weight.reshape(64, 2, n_lon, 64).transpose(0, 2, 1, 3).reshape(64, width)
    vmem = pl.BlockSpec(memory_space=pltpu.VMEM)
    grad_input, grad_weight = pl.pallas_call(
        functools.partial(kernel, sizes),
        out_shape=(
            jax.ShapeDtypeStruct((rows, nlon), BF16),
            jax.ShapeDtypeStruct((64, width), BF16),
        ),
        in_specs=[vmem] * 7,
        out_specs=(vmem, vmem),
        scratch_shapes=[
            pltpu.VMEM((4, n_lat, M_DEV * ROWS, 128), BF16),
            pltpu.VMEM((4, n_lat, M_DEV * ROWS, 128), BF16),
            pltpu.VMEM((4, n_deg, M_DEV, 128), BF16),
            pltpu.VMEM((4, n_deg, M_DEV, 128), BF16),
            pltpu.VMEM((orders, width), BF16),
            pltpu.VMEM((n_dp, n_lat, M_DEV, 128), BF16),
            pltpu.VMEM((n_dp, n_deg, M_DEV, 128), BF16),
            pltpu.VMEM((width, width), BF16),
            pltpu.VMEM((n_dp * orders, width), BF16),
            pltpu.VMEM((rows, nlon), BF16),
            pltpu.VMEM((max(n_deg * M_DEV, orders * ROWS), 128), F32),
            pltpu.VMEM((n_deg * 8, nlat), F32),
            pltpu.VMEM((M_DEV, n_deg, nlat), BF16),
            pltpu.VMEM((M_DEV, nlat, n_deg), BF16),
            pltpu.VMEM((M_DEV, n_deg, nlat), BF16),
            pltpu.VMEM((M_DEV, nlat, n_deg), BF16),
            pltpu.SemaphoreType.DMA((11,)),
            pltpu.SemaphoreType.DMA((11,)),
        ],
        compiler_params=pltpu.CompilerParams(
            collective_id=0, has_side_effects=True, vmem_limit_bytes=48 * 1024 * 1024
        ),
        name="block",
    )(
        field.reshape(rows, nlon),
        cotangent.reshape(rows, nlon),
        weights,
        forward,
        inverse,
        seeds,
        lat_rows,
    )
    grad_weight = grad_weight.reshape(64, n_lon, 2, 64).transpose(0, 2, 1, 3)
    return (
        grad_input.reshape(1, ROWS, SLAB, nlon),
        grad_weight.reshape(64, 1, 2, n_lon * SLAB),
    )


def solution(mesh):
    sizes = (mesh.shape["dp"], mesh.shape["lat"], mesh.shape["lon"])
    return jax.shard_map(
        functools.partial(body, sizes),
        mesh=mesh,
        in_specs=(
            P("dp", "lat", "lon", None),
            P("dp", "lat", "lon", None),
            P("dp", ("lat", "lon"), None, None),
        ),
        out_specs=(P("dp", "lat", "lon", None), P("dp", ("lat", "lon"), None, None)),
        check_vma=False,
    )
```

```python
import functools
import math

import jax
import jax.numpy as jnp
import numpy as np
from jax import lax
from jax.experimental import pallas as pl
from jax.experimental.pallas import tpu as pltpu
from jax.sharding import PartitionSpec as P

MESH = pl.DeviceIdType.MESH
BF16 = jnp.bfloat16
F32 = jnp.float32
M_DEV = 4
ROWS = 8
SLAB = 64
CHUNKS = 2
MC = M_DEV // CHUNKS
SEM_COEFF, SEM_GRADS, SEM_RESULT, SEM_RING = (8 * CHUNKS + i for i in range(4))


def fourier_tables(nlon, norders):
    cols = np.arange(nlon, dtype=np.int32)[None, :]
    rows = np.arange(norders, dtype=np.int32)[:, None]
    phase = (cols * rows % nlon).astype(np.float32) * np.float32(2.0 * math.pi / nlon)
    cosine, sine = np.cos(phase), np.sin(phase)
    doubled = np.where(rows == 0, 1.0, 2.0).astype(np.float32)
    forward = np.stack([cosine / np.float32(nlon), -sine / np.float32(nlon)])
    inverse = np.stack([doubled * cosine, -doubled * sine])

    def by_chunk(table):
        table = table.reshape(2, norders // M_DEV, CHUNKS, MC, nlon).transpose(2, 0, 1, 3, 4)
        return jnp.asarray(table.reshape(2 * norders, nlon), BF16)

    return by_chunk(forward), by_chunk(inverse)


def legendre_seeds(nlat, norders):
    theta = np.float32(math.pi) * (np.arange(nlat, dtype=np.float32) + np.float32(0.5)) / np.float32(nlat)
    theta = theta.astype(np.float64)
    seeds = np.zeros((norders // M_DEV, 8, nlat), np.float32)
    for m in range(norders):
        scale = math.lgamma(2.0 * m + 2.0) - m * math.log(4.0) - 2.0 * math.lgamma(m + 1.0)
        start = 0.5 * math.log(0.5) + 0.5 * scale + m * np.log(np.sin(theta))
        seeds[m // M_DEV, m % M_DEV] = np.exp(start).astype(np.float32)
    rows = np.zeros((8, nlat), np.float32)
    rows[0] = np.cos(theta)
    rows[1] = math.pi * np.sin(theta) / nlat
    return jnp.asarray(seeds.reshape(-1, nlat)), jnp.asarray(rows)


def swap_halves(tile):
    return pltpu.roll(tile, 64, axis=1)


def low_lanes(shape):
    return lax.broadcasted_iota(jnp.int32, shape, 1) < 64


def gelu_slope(values):
    return 0.5 * (1.0 + lax.erf(values * (1.0 / math.sqrt(2.0)))) + values * jnp.exp(
        -0.5 * values * values
    ) * (1.0 / math.sqrt(2.0 * math.pi))


def kernel(
    sizes,
    x_hbm,
    g_hbm,
    w_hbm,
    forward_hbm,
    inverse_hbm,
    seeds_hbm,
    rows_hbm,
    out_ref,
    gw_ref,
    by_lat_out,
    by_lat_in,
    by_deg_out,
    by_deg_in,
    wide,
    coeff_all,
    grads_all,
    mixing,
    coeff_t,
    result_out,
    result_in,
    combined,
    fgrad,
    stage,
    leg,
    analysis,
    analysis_t,
    synthesis,
    synthesis_t,
    x_ref,
    g_ref,
    w_ref,
    forward_ref,
    inverse_ref,
    seeds_ref,
    rows_ref,
    send_sem,
    recv_sem,
    load_sem,
):
    loads = [
        pltpu.make_async_copy(src, dst, load_sem.at[i])
        for i, (src, dst) in enumerate(
            (
                (x_hbm, x_ref),
                (forward_hbm, forward_ref),
                (w_hbm, w_ref),
                (seeds_hbm, seeds_ref),
                (rows_hbm, rows_ref),
                (inverse_hbm, inverse_ref),
                (g_hbm, g_ref),
            )
        )
    ]
    for load in loads:
        load.start()
    n_dp, n_lat, n_lon = sizes
    n_x = min(n_lon, 4)
    n_zlo = n_lat // 2
    n_z = n_zlo * (n_lon // n_x)
    orders = n_lat * M_DEV
    part_orders = orders // CHUNKS
    n_deg = n_lat * n_lon
    nlat = n_lat * ROWS
    hops = n_dp // 2
    s = lax.axis_index("dp")
    a = lax.axis_index("lat")
    y = lax.axis_index("lon")
    chip, core = lax.div(a, 2), lax.rem(a, 2)
    x, zhi = lax.rem(y, n_x), lax.div(y, n_x)
    z = zhi * n_zlo + chip

    def over_degree_group(visit):
        def step(k, carry):
            half = lax.div(k + 1, 2)
            off = jnp.where(lax.rem(k, 2) == 1, n_z // 2 - half, n_z // 2 + half)
            zt = lax.rem(z + off, n_z)
            zl, zh = lax.rem(zt, n_zlo), lax.div(zt, n_zlo)
            for dx in list(range(n_x // 2, 0, -1)) + list(range(n_x // 2 + 1, n_x)) + [0]:
                for dc in (1, 0):
                    la = zl * 2 + lax.rem(core + dc, 2)
                    lo = zh * n_x + lax.rem(x + dx, n_x)
                    if dx == 0 and dc == 0:
                        pl.when(k < n_z - 1)(functools.partial(visit, la, lo))
                    else:
                        visit(la, lo)
            return carry

        lax.fori_loop(0, n_z, step, 0)

    def over_lat_group(visit):
        for d in range(n_zlo - 1, 0, -1):
            for q in (chip + d, chip - d):

                @pl.when((q >= 0) & (q < n_zlo))
                def _(q=q):
                    visit(q * 2)
                    visit(q * 2 + 1)

        visit(chip * 2 + 1 - core)

    def over_dp_group(visit):
        for d in list(range(n_dp // 2, 0, -1)) + list(range(n_dp // 2 + 1, n_dp)):
            visit(lax.rem(s + d, n_dp))

    def remote(src, dst, sem, device):
        pltpu.make_async_remote_copy(
            src_ref=src,
            dst_ref=dst,
            send_sem=send_sem.at[sem],
            recv_sem=recv_sem.at[sem],
            device_id=device,
            device_id_type=MESH,
        ).start()

    def local(src, dst, sem):
        pltpu.make_async_copy(src, dst, recv_sem.at[sem]).start()

    def arrived(ref, sem):
        pltpu.make_async_copy(ref, ref, recv_sem.at[sem]).wait()

    def sent(ref, sem):
        pltpu.make_async_copy(ref, ref, send_sem.at[sem]).wait()

    def send_by_lat(e, k, h):
        src, dst, sem = by_lat_out.at[k, h], by_lat_in.at[k, h], e * CHUNKS + h
        over_lat_group(lambda j: remote(src.at[j], dst.at[a], sem, {"lat": j}))
        local(src.at[a], dst.at[a], sem)

    def send_to_degrees(e, k, h):
        src, dst, sem = by_deg_out.at[k, h], by_deg_in.at[k, h], e * CHUNKS + h
        mine = y * n_lat + a
        over_degree_group(
            lambda la, lo: remote(src.at[la * n_lon + lo], dst.at[mine], sem, {"lat": la, "lon": lo})
        )
        local(src.at[a * n_lon + y], dst.at[mine], sem)

    def send_to_orders(e, k, h):
        src, dst, sem = by_deg_out.at[k, h], by_deg_in.at[k, h], e * CHUNKS + h
        mine = a * n_lon + y
        over_degree_group(
            lambda la, lo: remote(src.at[lo * n_lat + la], dst.at[mine], sem, {"lat": la, "lon": lo})
        )
        local(src.at[y * n_lat + a], dst.at[mine], sem)

    def by_lat_arrived(e, k, h):
        arrived(by_lat_in.at[k, h], e * CHUNKS + h)

    def by_deg_arrived(e, k, h):
        arrived(by_deg_in.at[k, h], e * CHUNKS + h)

    def to_spectrum(table_ref, values_ref, k, h):
        out = lax.dot_general(
            table_ref[h * 2 * part_orders : (h + 1) * 2 * part_orders, :],
            values_ref[...],
            (((1,), (1,)), ((), ())),
            preferred_element_type=F32,
        )
        low = low_lanes((part_orders, 128))
        for j in range(ROWS // 2):
            real = out[:part_orders, j * 128 : (j + 1) * 128]
            imag = out[part_orders:, j * 128 : (j + 1) * 128]
            stage[pl.ds(2 * j, part_orders, stride=ROWS), :] = jnp.where(low, real, swap_halves(imag))
            stage[pl.ds(2 * j + 1, part_orders, stride=ROWS), :] = jnp.where(
                low, swap_halves(real), imag
            )
        by_lat_out[k, h] = (
            stage[: part_orders * ROWS, :].astype(BF16).reshape(n_lat, MC * ROWS, 128)
        )

    def to_degrees(tables, k, h):
        for m in range(MC):
            part = by_lat_in[k, h, :, m * ROWS : (m + 1) * ROWS, :]
            part = part.astype(F32).reshape(nlat, 128).astype(BF16)
            stage[pl.ds(m, n_deg, stride=MC), :] = jnp.dot(
                tables[h * MC + m], part, preferred_element_type=F32
            )
        return stage[: n_deg * MC, :].reshape(n_deg, MC, 128).astype(BF16)

    def gather_wide(k, h):
        for j in range(n_lon):
            part = by_deg_in[k, h, j * n_lat : (j + 1) * n_lat]
            wide[h, :, j * 128 : (j + 1) * 128] = (
                part.astype(F32).reshape(part_orders, 128).astype(BF16)
            )

    def scatter_wide(value, k, h):
        for j in range(n_lon):
            part = value[:, j * 128 : (j + 1) * 128].reshape(n_lat, MC, 128)
            by_deg_out[k, h, j * n_lat : (j + 1) * n_lat] = part.astype(BF16)

    def to_rows(tables, k_in, k, h):
        stage[: n_deg * MC, :] = by_deg_in[k_in, h].astype(F32).reshape(n_deg * MC, 128)
        parts = []
        for m in range(MC):
            part = stage[pl.ds(m, n_deg, stride=MC), :].astype(BF16)
            out = jnp.dot(tables[h * MC + m], part, preferred_element_type=F32)
            parts.append(out.reshape(n_lat, ROWS, 128))
        both = jnp.stack(parts, axis=1).reshape(n_lat, MC * ROWS, 128)
        by_lat_out[k, h] = both.astype(BF16)

    def combine(k, h):
        stage[: part_orders * ROWS, :] = by_lat_in[k, h].astype(F32).reshape(part_orders * ROWS, 128)
        low = low_lanes((part_orders, 128))
        for j in range(ROWS // 2):
            even = stage[pl.ds(2 * j, part_orders, stride=ROWS), :]
            odd = stage[pl.ds(2 * j + 1, part_orders, stride=ROWS), :]
            real = jnp.where(low, even, swap_halves(odd))
            imag = jnp.where(low, swap_halves(even), odd)
            combined[
                h * 2 * part_orders : (h + 1) * 2 * part_orders, j * 128 : (j + 1) * 128
            ] = jnp.concatenate([real, imag], axis=0).astype(BF16)

    def to_grid(table_ref, use):
        for j in range(ROWS // 2):
            rows = slice(j * 128, (j + 1) * 128)
            use(
                rows,
                lax.dot_general(
                    combined[:, rows],
                    table_ref[...],
                    (((0,), (0,)), ((), ())),
                    preferred_element_type=F32,
                ),
            )

    barrier = pltpu.get_barrier_semaphore()

    def greet(device):
        pl.semaphore_signal(barrier, inc=1, device_id=device, device_id_type=MESH)

    over_degree_group(lambda la, lo: greet({"lat": la, "lon": lo}))
    over_dp_group(lambda j: greet({"dp": j}))

    low = low_lanes((64, 128))

    def upper(block, start=0, size=64):
        return pl.ds(pl.multiple_of(block * 128 + start, 32), size)

    def fill_lower(block):
        rows = pl.ds(pl.multiple_of(block * 128 + 64, 64), 64)
        for i in range(n_lon):
            tile = slice(i * 128, (i + 1) * 128)
            turned = swap_halves(mixing[upper(block), tile].astype(F32))
            mixing[rows, tile] = jnp.where(low, -turned, turned).astype(BF16)

    right, left = lax.rem(s + 1, n_dp), lax.rem(s + n_dp - 1, n_dp)

    def from_left(k):
        return lax.rem(s + n_dp - k, n_dp)

    def from_right(k):
        return lax.rem(s + k, n_dp)

    def halves(k):
        return [
            (half, to_right, SEM_RING + (k * 2 + half) * 2 + to_right)
            for half in (0, 1)
            for to_right in (0, 1)
            if k < hops - 1 or half == to_right
        ]

    def pass_weights(k, half=None):
        for part, to_right, sem in halves(k):
            if half is None or part == half:
                block = from_left(k) if to_right else from_right(k)
                rows = mixing.at[upper(block, 32 * part, 32), :]
                remote(rows, rows, sem, {"dp": right if to_right else left})

    def weights_arrived(k, half):
        for part, _, sem in halves(k):
            if part == half:
                arrived(mixing.at[pl.ds(0, 32), :], sem)
        if k < hops - 1:
            pass_weights(k + 1, half)
        if half == 1:
            fill_lower(from_right(k + 1))
            if k < hops - 1:
                fill_lower(from_left(k + 1))

    loads[0].wait()
    loads[1].wait()
    for h in range(CHUNKS):
        to_spectrum(forward_ref, x_ref, 0, h)
    pl.semaphore_wait(barrier, n_deg - 1 + n_dp - 1)

    for h in range(CHUNKS):
        send_by_lat(0, 0, h)
    loads[2].wait()
    weights = w_ref[...].astype(F32)
    for i in range(n_lon // 2):
        real = weights[:, 0, i * 128 : (i + 1) * 128]
        imag = weights[:, 1, i * 128 : (i + 1) * 128]
        mixing[upper(s), 2 * i * 128 : (2 * i + 1) * 128] = jnp.where(
            low, real, swap_halves(imag)
        ).astype(BF16)
        mixing[upper(s), (2 * i + 1) * 128 : (2 * i + 2) * 128] = jnp.where(
            low, swap_halves(real), imag
        ).astype(BF16)
    pass_weights(0)
    fill_lower(s)

    for load in loads[3:]:
        load.wait()

    order = (a * M_DEV + lax.broadcasted_iota(jnp.int32, (8, nlat), 0)).astype(F32)
    order_sq = order * order
    cosine = jnp.broadcast_to(rows_ref[0:1, :], (8, nlat))
    start = seeds_ref[pl.ds(pl.multiple_of(a * 8, 8), 8), :]

    def advance(degree, carry):
        older, newer, deg = carry
        below = deg - 1.0
        scale_a = jnp.sqrt(
            jnp.maximum(4.0 * deg * deg - 1.0, 0.0) / jnp.maximum(deg * deg - order_sq, 1.0)
        )
        scale_b = jnp.sqrt(
            jnp.maximum(below * below - order_sq, 0.0)
            / jnp.maximum(4.0 * (below * below) - 1.0, 1.0)
        )
        general = scale_a * (cosine * newer - scale_b * older)
        value = jnp.where(deg < order, 0.0, jnp.where(deg == order, start, general))
        leg[pl.ds(pl.multiple_of(degree * 8, 8), 8), :] = value
        return newer, value, deg + 1.0

    zeros = start * 0.0
    lax.fori_loop(0, n_deg, advance, (zeros, zeros, zeros), unroll=8)
    for m in range(M_DEV):
        table = leg[pl.ds(m, n_deg, stride=8), :]
        weighted = table * rows_ref[1:2, :]
        synthesis[m] = table.astype(BF16)
        analysis[m] = weighted.astype(BF16)
        synthesis_t[m] = table.T.astype(BF16)
        analysis_t[m] = weighted.T.astype(BF16)

    for half in (0, 1):
        weights_arrived(0, half)
    for h in range(CHUNKS):
        by_lat_arrived(0, 0, h)
        by_deg_out[0, h] = to_degrees(analysis, 0, h)
        send_to_degrees(1, 0, h)
        if h == 0 and hops > 1:
            for half in (0, 1):
                weights_arrived(1, half)
    for k in range(2, hops):
        for half in (0, 1):
            weights_arrived(k, half)

    for h in range(CHUNKS):
        by_deg_arrived(1, 0, h)
        gather_wide(0, h)
        scatter_wide(jnp.dot(wide[h], mixing[...], preferred_element_type=F32), 1, h)
        send_to_orders(2, 1, h)

    for h in range(CHUNKS):
        coeff = by_deg_in.at[0, h]
        over_dp_group(lambda j: remote(coeff, coeff_all.at[s, h], SEM_COEFF, {"dp": j}))
        local(coeff, coeff_all.at[s, h], SEM_COEFF)

    for h in range(CHUNKS):
        by_deg_arrived(2, 1, h)
        to_rows(synthesis_t, 1, 1, h)
        send_by_lat(3, 1, h)
    for h in range(CHUNKS):
        by_lat_arrived(3, 1, h)
        combine(1, h)

    def slope(rows, filtered):
        fgrad[rows, :] = (g_ref[rows, :].astype(F32) * gelu_slope(filtered)).astype(BF16)

    to_grid(inverse_ref, slope)
    for h in range(CHUNKS):
        to_spectrum(inverse_ref, fgrad, 2, h)
        send_by_lat(4, 2, h)
    for h in range(CHUNKS):
        by_lat_arrived(4, 2, h)
        by_deg_out[2, h] = to_degrees(synthesis, 2, h)
        send_to_degrees(5, 2, h)

    arrived(coeff_all, SEM_COEFF)
    for j in range(n_lon):
        part = coeff_all[:, :, j * n_lat : (j + 1) * n_lat].astype(F32).reshape(n_dp * orders, 128)
        coeff_t[j * 128 : (j + 1) * 128, :] = part.T.astype(BF16)

    for h in range(CHUNKS):
        by_deg_arrived(5, 2, h)
        gather_wide(2, h)
        scatter_wide(
            lax.dot_general(
                wide[h], mixing[...], (((1,), (1,)), ((), ())), preferred_element_type=F32
            ),
            3,
            h,
        )
        send_to_orders(6, 3, h)

        def grads_block(j, h=h):
            return by_deg_in.at[2, h, pl.ds(j * n_lat, n_lat)]

        over_dp_group(lambda j: remote(grads_block(j), grads_all.at[s, h], SEM_GRADS, {"dp": j}))
        local(grads_block(s), grads_all.at[s, h], SEM_GRADS)

    for h in range(CHUNKS):
        by_deg_arrived(6, 3, h)
        to_rows(analysis_t, 3, 3, h)
        send_by_lat(7, 3, h)

    arrived(grads_all, SEM_GRADS)
    total = jnp.dot(
        coeff_t[...],
        grads_all[...].astype(F32).reshape(n_dp * orders, 128).astype(BF16),
        preferred_element_type=F32,
    )
    for j in range(n_lon):
        real = total[j * 128 : j * 128 + 64]
        imag = swap_halves(total[j * 128 + 64 : (j + 1) * 128])
        result_out[j] = (jnp.where(low, real + imag, real - imag) * (1.0 / n_dp)).astype(BF16)
    over_dp_group(lambda j: remote(result_out.at[j], result_in.at[s], SEM_RESULT, {"dp": j}))
    local(result_out.at[s], result_in.at[s], SEM_RESULT)

    for h in range(CHUNKS):
        by_lat_arrived(7, 3, h)
        combine(3, h)

    def finish(rows, branch):
        out_ref[rows, :] = branch

    to_grid(forward_ref, finish)

    arrived(result_in, SEM_RESULT)
    for i in range(n_lon // 2):
        even, odd = result_in[2 * i].astype(F32), result_in[2 * i + 1].astype(F32)
        both = jnp.stack(
            [jnp.where(low, even, swap_halves(odd)), jnp.where(low, swap_halves(even), odd)], axis=1
        )
        gw_ref[:, :, i * 128 : (i + 1) * 128] = both.astype(BF16)

    for h in range(CHUNKS):
        for e, k in ((0, 0), (3, 1), (4, 2), (7, 3)):
            sent(by_lat_out.at[k, h, pl.ds(0, n_lat - 1)], e * CHUNKS + h)
        for e, k in ((1, 0), (2, 1), (5, 2), (6, 3)):
            sent(by_deg_out.at[k, h, pl.ds(0, n_deg - 1)], e * CHUNKS + h)
    sent(coeff_all.at[pl.ds(0, n_dp - 1)], SEM_COEFF)
    sent(grads_all.at[pl.ds(0, n_dp - 1)], SEM_GRADS)
    sent(result_in.at[pl.ds(0, n_dp - 1)], SEM_RESULT)
    for k in range(hops):
        for _, _, sem in halves(k):
            sent(mixing.at[pl.ds(0, 32), :], sem)


def body(sizes, field, cotangent, spectral_weight):
    n_dp, n_lat, n_lon = sizes
    nlon = field.shape[3]
    orders, n_deg, nlat = n_lat * M_DEV, n_lat * n_lon, n_lat * ROWS
    width = n_lon * 128
    rows = ROWS * SLAB
    forward, inverse = fourier_tables(nlon, orders)
    seeds, lat_rows = legendre_seeds(nlat, orders)
    vmem = pl.BlockSpec(memory_space=pltpu.VMEM)
    hbm = pl.BlockSpec(memory_space=pltpu.HBM)
    operands = (
        field.reshape(rows, nlon),
        cotangent.reshape(rows, nlon),
        spectral_weight.reshape(64, 2, n_lon * SLAB),
        forward,
        inverse,
        seeds,
        lat_rows,
    )
    n_sem = 8 * CHUNKS + 3 + 2 * n_dp
    branch, grad_weight = pl.pallas_call(
        functools.partial(kernel, sizes),
        out_shape=(
            jax.ShapeDtypeStruct((rows, nlon), F32),
            jax.ShapeDtypeStruct((64, 2, n_lon * SLAB), BF16),
        ),
        in_specs=[hbm] * 7,
        out_specs=(vmem, vmem),
        scratch_shapes=[
            pltpu.VMEM((4, CHUNKS, n_lat, MC * ROWS, 128), BF16),
            pltpu.VMEM((4, CHUNKS, n_lat, MC * ROWS, 128), BF16),
            pltpu.VMEM((4, CHUNKS, n_deg, MC, 128), BF16),
            pltpu.VMEM((4, CHUNKS, n_deg, MC, 128), BF16),
            pltpu.VMEM((CHUNKS, orders // CHUNKS, width), BF16),
            pltpu.VMEM((n_dp, CHUNKS, n_deg, MC, 128), BF16),
            pltpu.VMEM((n_dp, CHUNKS, n_lat, MC, 128), BF16),
            pltpu.VMEM((width, width), BF16),
            pltpu.VMEM((width, n_dp * orders), BF16),
            pltpu.VMEM((n_dp, 64, 128), BF16),
            pltpu.VMEM((n_dp, 64, 128), BF16),
            pltpu.VMEM((2 * orders, rows), BF16),
            pltpu.VMEM((rows, nlon), BF16),
            pltpu.VMEM((max(n_deg * MC, orders * ROWS // CHUNKS), 128), F32),
            pltpu.VMEM((n_deg * 8, nlat), F32),
            pltpu.VMEM((M_DEV, n_deg, nlat), BF16),
            pltpu.VMEM((M_DEV, nlat, n_deg), BF16),
            pltpu.VMEM((M_DEV, n_deg, nlat), BF16),
            pltpu.VMEM((M_DEV, nlat, n_deg), BF16),
            *(pltpu.VMEM(operand.shape, operand.dtype) for operand in operands),
            pltpu.SemaphoreType.DMA((n_sem,)),
            pltpu.SemaphoreType.DMA((n_sem,)),
            pltpu.SemaphoreType.DMA((len(operands),)),
        ],
        compiler_params=pltpu.CompilerParams(
            collective_id=0, has_side_effects=True, vmem_limit_bytes=60 * 1024 * 1024
        ),
        name="block",
    )(*operands)
    return (
        (cotangent.astype(F32) + branch.reshape(cotangent.shape)).astype(BF16),
        grad_weight.reshape(64, 1, 2, n_lon * SLAB),
    )


def solution(mesh):
    sizes = (mesh.shape["dp"], mesh.shape["lat"], mesh.shape["lon"])
    return jax.shard_map(
        functools.partial(body, sizes),
        mesh=mesh,
        in_specs=(
            P("dp", "lat", "lon", None),
            P("dp", "lat", "lon", None),
            P("dp", ("lat", "lon"), None, None),
        ),
        out_specs=(P("dp", "lat", "lon", None), P("dp", ("lat", "lon"), None, None)),
        check_vma=False,
    )
```
